32 devices in a mesh: section: 2 (over x), dp: 4 (over z), shard: 4 (over y, core).
Axes of the slice: x: 2, y: 2, z: 4, core: 2. Of those that a mesh axis runs over, the one named last changes fastest.
Arguments:
- inputs: bfloat16 [32, 256, 2048], P(('dp', 'shard')), may hold values from -6 to 6
- segment_ids: int32 [32, 256], P(('dp', 'shard')), may hold values from 0 to 2, never falling along the last dimension, each value on 1 to 160 neighbouring positions
- w_query: bfloat16 [2, 2048, 2048], P('section', 'shard'), may hold values from -0.125 to 0.125
- w_key: bfloat16 [2, 2048, 256], P('section', 'shard'), may hold values from -0.125 to 0.125
- w_value: bfloat16 [2, 2048, 256], P('section', 'shard'), may hold values from -0.125 to 0.125
- w_out: bfloat16 [2, 2048, 2048], P('section', 'shard'), may hold values from -0.75 to 0.75
- w_gate: bfloat16 [2, 2048, 5632], P('section', 'shard'), may hold values from -0.125 to 0.125
- w_up: bfloat16 [2, 2048, 5632], P('section', 'shard'), may hold values from -0.125 to 0.125
- w_down: bfloat16 [2, 5632, 2048], P('section', 'shard'), may hold values from -0.078125 to 0.078125
- gain_attn: bfloat16 [2, 2048], P('section', 'shard'), may hold values from 0.099609375 to 1.8984375
- gain_ffn: bfloat16 [2, 2048], P('section', 'shard'), may hold values from 0.099609375 to 1.8984375
- cotangent: bfloat16 [32, 256, 2048], P(('dp', 'shard')), may hold values from -6 to 6
Outputs:
- acts: bfloat16 [2, 32, 256, 2048], P('section', ('dp', 'shard'))
- act_grads: bfloat16 [2, 32, 256, 2048], P('section', ('dp', 'shard'))
- grad_query: float32 [2, 2048, 2048], P('section', 'shard')
- grad_key: float32 [2, 2048, 256], P('section', 'shard')
- grad_value: float32 [2, 2048, 256], P('section', 'shard')
- grad_out: float32 [2, 2048, 2048], P('section', 'shard')
- grad_gate: float32 [2, 2048, 5632], P('section', 'shard')
- grad_up: float32 [2, 2048, 5632], P('section', 'shard')
- grad_down: float32 [2, 5632, 2048], P('section', 'shard')
- grad_gain_attn: float32 [2, 2048], P('section', 'shard')
- grad_gain_ffn: float32 [2, 2048], P('section', 'shard')
The draws below stay inside these ranges and needn't reach their ends.
Inputs may be any that keep to these rules, and one draw needn't show every extreme that they name: `segment_ids`: within each sequence the document numbers never fall; each of the 3 numbers covers 1 to 160 consecutive tokens, and one covers exactly 160.
All inputs are finite; a program needn't handle non-finite values.
Results may differ from the reference program's by a relative error of at most 0.025.
Values may be sent and summed in bfloat16 or wider, within the bound.
No kernel may reach another device: no remote copies, remote signals or barrier semaphores. Data moves between devices by JAX's collectives and lax.ppermute only.
A program may use at most 512 MiB of HBM per device.

```python
import math
import jax
import jax.numpy as jnp
import numpy as np
from jax import lax

D = 2048
HEADS = 32
KV_HEADS = 4
HEAD_DIM = 64
FF = 5632
KV_DIM = 256
SEQ_LEN = 256
DOCS = 3
MOST_DOC = 160
SEQS = 32


def block_levels(own_key, extent, cuts, smallest, high):
    level, own = 1.0, jax.random.fold_in(own_key, 6)
    for dim, shards_of in cuts:
        heights = jnp.exp(jax.random.uniform(jax.random.fold_in(own, dim), (shards_of,), jnp.float32, smallest / len(cuts), high / len(cuts)))
        level = level * jnp.repeat(heights, extent[dim] // shards_of).reshape([-1 if axis == dim else 1 for axis in range(len(extent))])
    return level


def profile(count, total, most, slope):
    loads = [(1 << 20) // math.isqrt(grade ** slope) + 1 for grade in range(2, count + 1)]
    spare, holding = total - most - (count - 1), [1] * (count - 1)
    while spare > 0:
        free = [i for i in range(count - 1) if holding[i] < most]
        mass, remaining = sum([loads[i] for i in free]), spare
        for i in free:
            extra = min(most - holding[i], max(1, remaining * loads[i] // mass), spare)
            holding[i] = holding[i] + extra
            spare = spare - extra
    return np.array([most] + holding)


def ragged_sizes(own_key, amount, total, reach, slope):
    if amount == 2:
        one = jax.random.randint(own_key, (), max(1, total - reach), min(reach, total - 1) + 1)
        return jnp.stack([one, total - one])
    sizes = jnp.asarray(profile(amount, total, reach, slope), jnp.int32)
    twos = (amount - 1) // 2
    source_of, receiver = sizes[1:1 + 2 * twos:2], sizes[2:2 + 2 * twos:2]
    room = jnp.minimum(source_of - 1, reach - receiver)
    moved = jax.random.randint(jax.random.fold_in(own_key, 1), (twos,), 0, 1 << 20) % (room + 1)
    sizes = sizes.at[1:1 + 2 * twos:2].set(source_of - moved).at[2:2 + 2 * twos:2].set(receiver + moved)
    return sizes[jax.random.permutation(jax.random.fold_in(own_key, 2), amount)]


def normal_values(rng, dims, scale, reach, cuts=(), kind=jnp.bfloat16):
    factor_of = block_levels(rng, dims, cuts, -0.22, 0.18) if cuts else 1.0
    drawn = jax.random.normal(rng, dims, jnp.float32) * scale * factor_of
    return jnp.minimum(jnp.maximum(drawn, -reach), reach).astype(kind)


def setup_inputs(seed: int = 0) -> dict:
    streams_of = jax.random.split(jax.random.key(seed), 13)
    return {
        "inputs": normal_values(streams_of[0], (SEQS, SEQ_LEN, D), 1.0, 6.0, ((0, 16),)),
        "segment_ids": jax.vmap(lambda own: jnp.searchsorted(jnp.cumsum(ragged_sizes(own, DOCS, SEQ_LEN, MOST_DOC, 1)), jnp.arange(SEQ_LEN), side="right"))(jax.random.split(streams_of[1], SEQS)).reshape((SEQS, SEQ_LEN)).astype(jnp.int32),
        "w_query": normal_values(streams_of[2], (2, D, D), D ** -0.5, 0.125, ((0, 2), (1, 4))),
        "w_key": normal_values(streams_of[3], (2, D, KV_DIM), D ** -0.5, 0.125, ((0, 2), (1, 4))),
        "w_value": normal_values(streams_of[4], (2, D, KV_DIM), D ** -0.5, 0.125, ((0, 2), (1, 4))),
        "w_out": normal_values(streams_of[5], (2, D, D), (D // 32) ** -0.5, 0.75, ((0, 2), (1, 4))),
        "w_gate": normal_values(streams_of[6], (2, D, FF), D ** -0.5, 0.125, ((0, 2), (1, 4))),
        "w_up": normal_values(streams_of[7], (2, D, FF), D ** -0.5, 0.125, ((0, 2), (1, 4))),
        "w_down": normal_values(streams_of[8], (2, FF, D), FF ** -0.5, 0.078125, ((0, 2), (1, 4))),
        "gain_attn": jnp.clip(1.0 + 0.18 * jax.random.normal(streams_of[9], (2, D), jnp.float32), 0.099609375, 1.8984375).astype(jnp.bfloat16),
        "gain_ffn": jnp.clip(1.0 + 0.18 * jax.random.normal(streams_of[10], (2, D), jnp.float32), 0.099609375, 1.8984375).astype(jnp.bfloat16),
        "cotangent": normal_values(streams_of[11], (SEQS, SEQ_LEN, D), 1.0, 6.0, ((0, 16),)),
    }


epsilon = 1e-05
highest = lax.Precision.HIGHEST

@jax.custom_vjp
def low(v):
    return lax.optimization_barrier(v.astype(jnp.bfloat16)).astype(jnp.float32)

@jax.custom_vjp
def low_back(v):
    return v

def low_keep(v):
    return (low(v), None)

def low_pass(kept, grad):
    return (grad,)

def back_keep(v):
    return (v, None)

def back_low(kept, grad):
    return (low(grad),)
low.defvjp(low_keep, low_pass)
low_back.defvjp(back_keep, back_low)

def matmul(left_side, right_side):
    return jnp.einsum('...i,ij->...j', left_side, right_side, precision=highest)

def rms_scale(values, gain_vector):
    inverse = lax.rsqrt(lax.optimization_barrier(jnp.mean(values * values, axis=-1, keepdims=True)) + epsilon)
    return values * inverse * gain_vector

def rotate(values, cosine, sine_table):
    half_dim = HEAD_DIM // 2
    turned = jnp.concatenate([-values[..., half_dim:], values[..., :half_dim]], axis=-1)
    return values * cosine[:, :, None, :] + turned * sine_table[:, :, None, :]

def rope_tables(segment_ids):
    length = segment_ids.shape[-1]
    places = jnp.arange(length, dtype=jnp.int32)
    same_doc = segment_ids[:, :, None] == segment_ids[:, None, :]
    earlier = places[None, :] < places[:, None]
    positions = lax.optimization_barrier(jnp.sum((same_doc & earlier[None]).astype(jnp.int32), axis=-1))
    allowed = same_doc & (places[None, :] <= places[:, None])[None]
    frequency = 10000.0 ** (-(jnp.arange(HEAD_DIM // 2, dtype=jnp.float32) * (2.0 / HEAD_DIM)))
    angles = positions.astype(jnp.float32)[..., None] * frequency
    angles = jnp.concatenate([angles, angles], axis=-1)
    return (jnp.cos(angles), jnp.sin(angles), allowed)

def attend_one(pieces):
    queries, keys, values, allowed = pieces
    length = queries.shape[0]
    grouped = queries.reshape(length, KV_HEADS, HEADS // KV_HEADS, HEAD_DIM)
    raw_scores = low_back(jnp.einsum('ikgd,jkd->kgij', grouped, keys, precision=highest))
    scores = jnp.where(allowed[None, None], raw_scores * HEAD_DIM ** (-0.5), -1000000000.0)
    attn_probs = low(jax.nn.softmax(scores, axis=-1))
    mixed = jnp.einsum('kgij,jkd->ikgd', attn_probs, values, precision=highest)
    return mixed.reshape(length, HEADS * HEAD_DIM)

def block_layer(hidden, weights, cosine, sine_table, allowed):
    w_query, w_key, w_value, w_out, w_gate, w_up, w_down, gain_attn, gain_ffn = weights
    seq_count, length, width = hidden.shape
    normed = low(rms_scale(hidden, gain_attn))
    query_proj = low_back(matmul(normed, w_query)).reshape(seq_count, length, HEADS, HEAD_DIM)
    queries = low(rotate(query_proj, cosine, sine_table))
    key_proj = low_back(matmul(normed, w_key)).reshape(seq_count, length, KV_HEADS, HEAD_DIM)
    keys = low(rotate(key_proj, cosine, sine_table))
    values = low(low_back(matmul(normed, w_value))).reshape(seq_count, length, KV_HEADS, HEAD_DIM)
    mixed = low(low_back(lax.map(jax.checkpoint(attend_one), (queries, keys, values, allowed))))
    middle = hidden + low_back(matmul(mixed, w_out))
    normed_ffn = low(rms_scale(middle, gain_ffn))
    gate_proj = low_back(matmul(normed_ffn, w_gate))
    upward = low_back(matmul(normed_ffn, w_up))
    inner_act = low(jax.nn.silu(gate_proj) * upward)
    return middle + low_back(matmul(inner_act, w_down))

def reference(inputs, segment_ids, w_query, w_key, w_value, w_out, w_gate, w_up, w_down, gain_attn, gain_ffn, cotangent):
    cosine, sine_table, allowed = rope_tables(segment_ids)
    stacked = tuple((member.astype(jnp.float32) for member in (w_query, w_key, w_value, w_out, w_gate, w_up, w_down, gain_attn, gain_ffn)))
    start_act = inputs.astype(jnp.float32)
    probe_zero = jnp.zeros_like(start_act)

    def full_pass(start_value, stacked_value, probe_value):
        layer_one = tuple((member[0] for member in stacked_value))
        layer_two = tuple((member[1] for member in stacked_value))
        first_out = block_layer(start_value, layer_one, cosine, sine_table, allowed)
        passed = low(low_back(first_out)) + probe_value
        return (block_layer(passed, layer_two, cosine, sine_table, allowed), first_out)
    final_out, pullback, first_out = jax.vjp(full_pass, start_act, stacked, probe_zero, has_aux=True)
    grad_start, grad_stacked, grad_probe = pullback(cotangent.astype(jnp.float32))
    acts = jnp.stack([first_out, final_out]).astype(jnp.bfloat16)
    act_grads = jnp.stack([grad_start, grad_probe]).astype(jnp.bfloat16)
    return (acts, act_grads, grad_stacked[0], grad_stacked[1], grad_stacked[2], grad_stacked[3], grad_stacked[4], grad_stacked[5], grad_stacked[6], grad_stacked[7], grad_stacked[8])
```

```python
import functools

import jax
import jax.numpy as jnp
from jax import lax
from jax.experimental import pallas as pl
from jax.experimental.pallas import tpu as pltpu
from jax.sharding import PartitionSpec as P

KV_HEADS = 4
HEAD_DIM = 64
GROUP = 8
PAIR = 2 * HEAD_DIM
EPSILON = 1e-05
BF16 = jnp.bfloat16
F32 = jnp.float32


def params(*semantics):
    return pltpu.CompilerParams(dimension_semantics=semantics, vmem_limit_bytes=60 * 1024 * 1024)


def cost(flops, nbytes):
    return pl.CostEstimate(flops=flops, bytes_accessed=nbytes, transcendentals=0)


def dot(left, right, left_dim=1, right_dim=0):
    dims = (((left_dim,), (right_dim,)), ((), ()))
    return lax.dot_general(left, right, dims, preferred_element_type=F32)


def matmul(left, right):
    return dot(left, right)


def back(grads, weight):
    return dot(grads, weight, 1, 1)


def term(left, right):
    return dot(left, right, 0, 0).astype(BF16)


def lanes(shape):
    return lax.broadcasted_iota(jnp.int32, shape, len(shape) - 1)


def turn(values, cosine, sine):
    first = lanes(values.shape) % HEAD_DIM < HEAD_DIM // 2
    up = pltpu.roll(values, PAIR - HEAD_DIM // 2, 1)
    down = pltpu.roll(values, HEAD_DIM // 2, 1)
    return values * cosine + jnp.where(first, -up, down) * sine


def turn_back(values, cosine, sine):
    first = lanes(values.shape) % HEAD_DIM < HEAD_DIM // 2
    scaled = values * sine
    up = pltpu.roll(scaled, PAIR - HEAD_DIM // 2, 1)
    down = pltpu.roll(scaled, HEAD_DIM // 2, 1)
    return values * cosine + jnp.where(first, up, -down)


def doubled(ref, head):
    block = ref[:, pl.ds(pl.multiple_of(head // 2 * PAIR, PAIR), PAIR)].astype(F32)
    mine = (lanes(block.shape) < HEAD_DIM) == (head % 2 == 0)
    return jnp.where(mine, block, pltpu.roll(block, HEAD_DIM, 1))


def stacked(ref):
    low = lanes((ref.shape[0], PAIR)) < HEAD_DIM
    parts = []
    for pair in range(GROUP // 2):
        block = ref[:, pair * PAIR : (pair + 1) * PAIR].astype(F32)
        parts.append(jnp.where(low, block, 0.0).astype(BF16))
        parts.append(jnp.where(low, 0.0, block).astype(BF16))
    return jnp.concatenate(parts, axis=0)


def masked_scores(queries, keys, row_segments, column_segments):
    length = keys.shape[0]
    raw = dot(queries, keys, 1, 1).reshape(GROUP, length, length) * HEAD_DIM**-0.5
    rows = lax.broadcasted_iota(jnp.int32, (length, length), 0)
    allowed = (row_segments == column_segments) & (lanes((length, length)) <= rows)
    scores = jnp.where(allowed[None], raw, -1e9)
    expanded = jnp.exp(scores - jnp.max(scores, axis=-1, keepdims=True))
    return expanded / jnp.sum(expanded, axis=-1, keepdims=True)


def attend_kernel(q_ref, k_ref, v_ref, cos_ref, sin_ref, row_ref, col_ref, *outs):
    mixed_ref, query_ref, key_ref, value_ref = outs
    head = pl.program_id(1)
    cosine, sine = cos_ref[...], sin_ref[...]

    @pl.when(head == 0)
    def _():
        for pair in range(KV_HEADS // 2):
            at = slice(pair * PAIR, (pair + 1) * PAIR)
            key_ref[:, at] = turn(k_ref[:, at], cosine, sine).astype(BF16)
            value_ref[:, at] = v_ref[:, at].astype(BF16)

    for pair in range(GROUP // 2):
        at = slice(pair * PAIR, (pair + 1) * PAIR)
        query_ref[:, at] = turn(q_ref[:, at], cosine, sine).astype(BF16)
    keys = doubled(key_ref, head).astype(BF16)
    values = doubled(value_ref, head)
    length = keys.shape[0]
    low = lanes(values.shape) < HEAD_DIM
    low_values = jnp.where(low, values, 0.0).astype(BF16)
    high_values = jnp.where(low, 0.0, values).astype(BF16)
    probs = masked_scores(stacked(query_ref), keys, row_ref[...], col_ref[0]).astype(BF16)
    for pair in range(GROUP // 2):
        both = dot(probs[2 * pair], low_values) + dot(probs[2 * pair + 1], high_values)
        mixed_ref[:, pair * PAIR : (pair + 1) * PAIR] = both.astype(BF16)


def attend(projected, table):
    cosine, sine, row_segments, column_segments = table
    seqs = column_segments.shape[0]
    length = column_segments.shape[2]
    tokens = seqs * length
    width = GROUP * HEAD_DIM
    keys = KV_HEADS * HEAD_DIM
    whole = pl.BlockSpec((length, keys), lambda s, g: (s, 0))
    heads = pl.BlockSpec((length, width), lambda s, g: (s, g))
    tables = pl.BlockSpec((length, PAIR), lambda s, g: (s, 0))
    first_key = KV_HEADS * width // keys
    return pl.pallas_call(
        attend_kernel,
        name="attend",
        grid=(seqs, KV_HEADS),
        in_specs=[
            heads,
            pl.BlockSpec((length, keys), lambda s, g: (s, first_key)),
            pl.BlockSpec((length, keys), lambda s, g: (s, first_key + 1)),
            tables,
            tables,
            pl.BlockSpec((length, 1), lambda s, g: (s, 0)),
            pl.BlockSpec((1, 1, length), lambda s, g: (s, 0, 0)),
        ],
        out_specs=[heads, heads, whole, whole],
        out_shape=[
            jax.ShapeDtypeStruct((tokens, KV_HEADS * width), BF16),
            jax.ShapeDtypeStruct((tokens, KV_HEADS * width), BF16),
            jax.ShapeDtypeStruct((tokens, keys), BF16),
            jax.ShapeDtypeStruct((tokens, keys), BF16),
        ],
        compiler_params=params("arbitrary", "arbitrary"),
        cost_estimate=cost(8 * tokens * length * KV_HEADS * width, 16 * tokens * KV_HEADS * width),
    )(projected, projected, projected, cosine, sine, row_segments, column_segments)


def attend_back_kernel(d_ref, query_ref, key_ref, value_ref, cos_ref, sin_ref, row_ref, col_ref, *outs):
    dq_ref, dk_ref, dv_ref = outs
    head = pl.program_id(1)
    cosine, sine = cos_ref[...], sin_ref[...]
    keys = doubled(key_ref, head)
    values = doubled(value_ref, head).astype(BF16)
    length = keys.shape[0]
    low = lanes(keys.shape) < HEAD_DIM
    low_keys = jnp.where(low, keys, 0.0).astype(BF16)
    high_keys = jnp.where(low, 0.0, keys).astype(BF16)
    queries = stacked(query_ref)
    given = stacked(d_ref)
    probs = masked_scores(queries, keys.astype(BF16), row_ref[...], col_ref[0])
    d_probs = dot(given, values, 1, 1).reshape(GROUP, length, length)
    delta = jnp.sum(probs * d_probs, axis=-1, keepdims=True)
    d_raw = (probs * (d_probs - delta) * HEAD_DIM**-0.5).astype(BF16)
    for pair in range(GROUP // 2):
        both = dot(d_raw[2 * pair], low_keys) + dot(d_raw[2 * pair + 1], high_keys)
        at = slice(pair * PAIR, (pair + 1) * PAIR)
        dq_ref[:, at] = turn_back(both, cosine, sine).astype(BF16)
    rows = GROUP * length
    d_key = dot(d_raw.reshape(rows, length), queries, 0, 0)
    d_value = dot(probs.astype(BF16).reshape(rows, length), given, 0, 0)
    d_key = turn_back(d_key + pltpu.roll(d_key, HEAD_DIM, 1), cosine, sine)
    d_value = d_value + pltpu.roll(d_value, HEAD_DIM, 1)
    at = pl.ds(pl.multiple_of(head // 2 * PAIR, PAIR), PAIR)
    keep = low & (head % 2 == 1)
    dk_ref[:, at] = jnp.where(keep, dk_ref[:, at].astype(F32), d_key).astype(BF16)
    dv_ref[:, at] = jnp.where(keep, dv_ref[:, at].astype(F32), d_value).astype(BF16)


def attend_back(d_mixed, query, key, value, table):
    cosine, sine, row_segments, column_segments = table
    seqs = column_segments.shape[0]
    length = column_segments.shape[2]
    width = GROUP * HEAD_DIM
    keys = KV_HEADS * HEAD_DIM
    whole = pl.BlockSpec((length, keys), lambda s, g: (s, 0))
    heads = pl.BlockSpec((length, width), lambda s, g: (s, g))
    tables = pl.BlockSpec((length, PAIR), lambda s, g: (s, 0))
    return pl.pallas_call(
        attend_back_kernel,
        name="attend_back",
        grid=(seqs, KV_HEADS),
        in_specs=[
            heads,
            heads,
            whole,
            whole,
            tables,
            tables,
            pl.BlockSpec((length, 1), lambda s, g: (s, 0)),
            pl.BlockSpec((1, 1, length), lambda s, g: (s, 0, 0)),
        ],
        out_specs=[heads, whole, whole],
        out_shape=[
            jax.ShapeDtypeStruct(query.shape, BF16),
            jax.ShapeDtypeStruct(key.shape, BF16),
            jax.ShapeDtypeStruct(key.shape, BF16),
        ],
        compiler_params=params("arbitrary", "arbitrary"),
        cost_estimate=cost(20 * query.size * length, 12 * query.size),
    )(d_mixed, query, key, value, cosine, sine, row_segments, column_segments)


def tile_of(size, most):
    return max(t for t in range(128, most + 1, 128) if size % t == 0)


def feed_kernel(x_ref, gate_ref, up_ref, *outs):
    gate = dot(x_ref[...], gate_ref[...])
    upward = dot(x_ref[...], up_ref[...])
    outs[0][...] = (gate * jax.nn.sigmoid(gate) * upward).astype(BF16)
    if len(outs) > 1:
        outs[1][...] = gate.astype(BF16)
        outs[2][...] = upward.astype(BF16)


def feed(normed, w_gate, w_up, kept):
    tokens, width = normed.shape
    size = w_gate.shape[1]
    tile = tile_of(size, 512)
    column = pl.BlockSpec((width, tile), lambda j: (0, j))
    out = pl.BlockSpec((tokens, tile), lambda j: (0, j))
    count = 3 if kept else 1
    return pl.pallas_call(
        feed_kernel,
        name="feed",
        grid=(size // tile,),
        in_specs=[pl.BlockSpec((tokens, width), lambda j: (0, 0)), column, column],
        out_specs=[out] * count,
        out_shape=[jax.ShapeDtypeStruct((tokens, size), BF16)] * count,
        compiler_params=params("arbitrary"),
        cost_estimate=cost(4 * tokens * width * size, 4 * width * size + 2 * count * tokens * size),
    )(normed, w_gate, w_up)


def feed_back_kernel(x_ref, down_ref, gate_ref, up_ref, dg_ref, de_ref):
    d_inner = dot(x_ref[...], down_ref[...], 1, 1)
    gate, upward = gate_ref[...].astype(F32), up_ref[...].astype(F32)
    sigmoid = jax.nn.sigmoid(gate)
    dg_ref[...] = (d_inner * upward * (sigmoid * (1.0 + gate * (1.0 - sigmoid)))).astype(BF16)
    de_ref[...] = (d_inner * (gate * sigmoid)).astype(BF16)


def feed_back(down_in, w_down, gate, upward):
    tokens, width = down_in.shape
    size = w_down.shape[0]
    tile = tile_of(size, 512)
    out = pl.BlockSpec((tokens, tile), lambda j: (0, j))
    return pl.pallas_call(
        feed_back_kernel,
        name="feed_back",
        grid=(size // tile,),
        in_specs=[
            pl.BlockSpec((tokens, width), lambda j: (0, 0)),
            pl.BlockSpec((tile, width), lambda j: (j, 0)),
            out,
            out,
        ],
        out_specs=[out, out],
        out_shape=[jax.ShapeDtypeStruct((tokens, size), BF16)] * 2,
        compiler_params=params("arbitrary"),
        cost_estimate=cost(2 * tokens * width * size, 2 * width * size + 8 * tokens * size),
    )(down_in, w_down, gate, upward)


def enter_back_kernel(dg_ref, de_ref, gate_ref, up_ref, out_ref):
    out_ref[...] = dot(dg_ref[...], gate_ref[...], 1, 1) + dot(de_ref[...], up_ref[...], 1, 1)


def enter_back(d_gate, d_up, w_gate, w_up):
    tokens, size = d_gate.shape
    width = w_gate.shape[0]
    tile = tile_of(width, 256)
    row = pl.BlockSpec((tile, size), lambda j: (j, 0))
    whole = pl.BlockSpec((tokens, size), lambda j: (0, 0), pipeline_mode=pl.Buffered(1))
    return pl.pallas_call(
        enter_back_kernel,
        name="enter_back",
        grid=(width // tile,),
        in_specs=[whole, whole, row, row],
        out_specs=pl.BlockSpec((tokens, tile), lambda j: (0, j)),
        out_shape=jax.ShapeDtypeStruct((tokens, width), F32),
        compiler_params=params("arbitrary"),
        cost_estimate=cost(4 * tokens * width * size, 4 * width * size + 4 * tokens * size),
    )(d_gate, d_up, w_gate, w_up)


def leave_kernel(inner_ref, down_ref, middle_ref, out_ref):
    out_ref[...] = (middle_ref[...] + dot(inner_ref[...], down_ref[...])).astype(BF16)


def leave(inner, w_down, middle):
    tokens, size = inner.shape
    width = w_down.shape[1]
    tile = tile_of(width, 256)
    out = pl.BlockSpec((tokens, tile), lambda j: (0, j))
    whole = pl.BlockSpec((tokens, size), lambda j: (0, 0), pipeline_mode=pl.Buffered(1))
    return pl.pallas_call(
        leave_kernel,
        name="leave",
        grid=(width // tile,),
        in_specs=[whole, pl.BlockSpec((size, tile), lambda j: (0, j)), out],
        out_specs=out,
        out_shape=jax.ShapeDtypeStruct((tokens, width), BF16),
        compiler_params=params("arbitrary"),
        cost_estimate=cost(2 * tokens * width * size, 2 * width * size + 4 * tokens * size),
    )(inner, w_down, middle)


def tables_of(segments):
    length = segments.shape[-1]
    places = jnp.arange(length, dtype=jnp.int32)
    same_doc = segments[:, :, None] == segments[:, None, :]
    earlier = places[None, :] < places[:, None]
    positions = jnp.sum((same_doc & earlier).astype(jnp.int32), axis=-1).reshape(-1, 1)
    frequency = 10000.0 ** (-(jnp.arange(HEAD_DIM // 2, dtype=F32) * (2.0 / HEAD_DIM)))
    angles = positions.astype(F32) * jnp.tile(frequency, 4)
    return jnp.cos(angles), jnp.sin(angles), segments.reshape(-1, 1), segments[:, None, :]


def normed_of(hidden, gain):
    inverse = lax.rsqrt(jnp.mean(hidden * hidden, axis=-1, keepdims=True) + EPSILON)
    unit = hidden * inverse
    return unit, inverse, (unit * gain).astype(BF16)


def through_norm(upstream, d_normed, unit, inverse, gain):
    d_unit = d_normed * gain
    return upstream + inverse * (d_unit - unit * jnp.mean(d_unit * unit, axis=-1, keepdims=True))


def attention_layer(entering, w_qkv, w_out, gain_attn, gain_ffn, table):
    unit, inverse, normed = normed_of(entering, gain_attn)
    mixed, query, key, value = attend(matmul(normed, w_qkv), table)
    middle = entering + matmul(mixed, w_out)
    return middle, normed_of(middle, gain_ffn)[2], (unit, inverse, normed, query, key, value, mixed)


def blank(shape, name):
    return pl.pallas_call(
        lambda out_ref: None,
        name=name,
        out_specs=pl.BlockSpec(memory_space=pl.ANY),
        out_shape=jax.ShapeDtypeStruct(shape, BF16),
        compiler_params=pltpu.CompilerParams(has_side_effects=True),
    )()


def put(whole, part, row, column=0):
    return lax.dynamic_update_slice(whole, part, (row, column))


class Sequence:
    def __init__(self):
        self.last = None

    def __call__(self, step, *operands):
        if self.last is not None:
            operands, _ = lax.optimization_barrier((operands, self.last))
        result = step(*operands)
        self.last = result
        return result


def ordered(value, own):
    width = value.shape[1] // 4
    blocks = [lax.dynamic_slice_in_dim(value, (own ^ j) * width, width, 1) for j in (0, 2, 1, 3)]
    return jnp.concatenate(blocks[:2], axis=1), jnp.concatenate(blocks[2:], axis=1)


def core(value):
    return lax.ppermute(value, "shard", [(s, s ^ 1) for s in range(4)])


def chip(value):
    return lax.ppermute(value, "shard", [(s, s ^ 2) for s in range(4)])


def along(value):
    return lax.ppermute(value, "dp", [(z, z ^ 1) for z in range(4)])


def added(*values):
    return sum(value.astype(F32) for value in values).astype(BF16)


class Chunk:
    def __init__(self, run, middle):
        self.run, self.middle = run, middle

    def terms(self, keep_left, send_left, right):
        self.sent = self.run(term, send_left, right)
        self.received = core(self.sent)
        self.keep = self.run(term, keep_left, right)

    def given(self, keep, sent):
        self.received = core(sent)
        self.keep = keep

    def to_chip(self):
        rows = self.keep.shape[0] // 2
        self.passed = chip(self.run(lambda k, r: added(k[rows:], r[rows:]), self.keep, self.received))

    def to_middle(self):
        rows = self.keep.shape[0] // 2
        self.value = self.run(
            lambda k, r, p: added(k[:rows], r[:rows], p), self.keep, self.received, self.passed
        )
        self.outer = lax.ppermute(self.value, "dp", [(0, 1), (3, 2)])

    def across(self):
        self.half = self.run(added, self.value, self.outer)
        self.other = lax.ppermute(self.half, "dp", [(1, 2), (2, 1)])

    def outward(self):
        self.whole = self.run(added, self.half, self.other)
        self.back = lax.ppermute(self.whole, "dp", [(1, 0), (2, 3)])

    def result(self):
        return jnp.where(self.middle, self.whole, self.back).astype(F32)


def paired_gather(run, w_query, w_side, w_out, w_gate, w_up, w_down):
    own = lax.axis_index("shard")
    odd = lax.axis_index("dp") % 2 == 1
    rows, feet = w_query.shape[0], w_down.shape[0]
    width, size = w_query.shape[1], w_gate.shape[1]
    half, quarter = rows // 2, feet // 4
    choose = lambda a, b: jnp.where(odd, a, b)
    side = chip(w_side)
    near = [chip(run(choose, w_out, w_query))]
    for i in (0, half):
        near.append(chip(run(choose, w_up[i : i + half], w_gate[i : i + half])))
    for i in (0, 2 * quarter):
        near.append(chip(run(choose, w_down[i + quarter : i + 2 * quarter], w_down[i : i + quarter])))
    owns = [core(array) for array in (w_side, w_query, w_out, w_gate, w_up, w_down)]
    far, near_core, far_core = {}, {}, {}

    def mine(name, array, other, shape, column=0):
        whole = blank(shape, name) if isinstance(name, str) else name
        size = array.shape[0]

        def step(whole, array, other):
            return put(put(whole, array, own * size, column), other, (own ^ 1) * size, column)

        return run(step, whole, array, other)

    def pass_on(i):
        value = run(lambda v: v, near[i])
        far[i] = along(value)
        near_core[i] = core(value)

    def arrive(i):
        value = run(lambda v: v, far[i])
        far[i] = value
        far_core[i] = core(value)

    def theirs(whole, i, wanted_odd, start, size, column=0):
        def step(whole, near, far, near_other, far_other):
            if wanted_odd:
                near, far, near_other, far_other = far, near, far_other, near_other
            whole = put(whole, jnp.where(odd, far, near), (own ^ 2) * size + start, column)
            return put(whole, jnp.where(odd, far_other, near_other), (own ^ 3) * size + start, column)

        return run(step, whole, near[i], far[i], near_core[i], far_core[i])

    qkv = mine("blank_qkv", w_side, owns[0], (4 * rows, width + w_side.shape[1]), width)
    qkv = mine(qkv, w_query, owns[1], None)
    out = mine("blank_out", w_out, owns[2], (4 * rows, width))
    side_core = core(side)
    qkv = run(
        lambda w, a, b: put(put(w, a, (own ^ 2) * rows, width), b, (own ^ 3) * rows, width),
        qkv,
        side,
        side_core,
    )
    pass_on(0)
    gate = mine("blank_gate", w_gate, owns[3], (4 * rows, size))
    upward = mine("blank_up", w_up, owns[4], (4 * rows, size))
    down = mine("blank_down", w_down, owns[5], (4 * feet, width))
    arrive(0)
    pass_on(1)
    qkv = theirs(qkv, 0, False, 0, rows)
    out = theirs(out, 0, True, 0, rows)
    yield qkv, out
    arrive(1)
    pass_on(2)
    gate = theirs(gate, 1, False, 0, rows)
    upward = theirs(upward, 1, True, 0, rows)
    pass_on(3)
    pass_on(4)
    arrive(2)
    gate = theirs(gate, 2, False, half, rows)
    upward = theirs(upward, 2, True, half, rows)
    yield gate, upward
    arrive(3)
    down = theirs(down, 3, False, 0, feet)
    down = theirs(down, 3, True, quarter, feet)
    arrive(4)
    down = theirs(down, 4, False, 2 * quarter, feet)
    down = theirs(down, 4, True, 3 * quarter, feet)
    yield down


def plain_gather(run, w_query, w_side, w_out, w_gate, w_up, w_down):
    whole = [
        lax.all_gather(array, "shard", axis=0, tiled=True)
        for array in (jnp.concatenate([w_query, w_side], axis=1), w_out, w_gate, w_up, w_down)
    ]
    yield whole[0], whole[1]
    yield whole[2], whole[3]
    yield whole[4]


def body(
    inputs, segment_ids, w_query, w_key, w_value, w_out, w_gate, w_up, w_down, gain_attn, gain_ffn, cotangent
):
    first_section = lax.axis_index("section") == 0
    paired = lax.axis_size("shard") == 4 and lax.axis_size("dp") == 4
    run = Sequence()
    seqs, length, width = inputs.shape
    tokens = seqs * length
    keys = w_key.shape[2]
    rows = w_query.shape[1]
    padding = jnp.zeros((rows, PAIR - 2), BF16)
    w_side = jnp.concatenate(
        [w_key[0], w_value[0], gain_attn[0][:, None], gain_ffn[0][:, None], padding], axis=1
    )
    arriving = (paired_gather if paired else plain_gather)(
        run, w_query[0], w_side, w_out[0], w_gate[0], w_up[0], w_down[0]
    )
    table = tables_of(segment_ids)
    own_input = inputs.reshape(tokens, width)
    own_grad = cotangent.reshape(tokens, width)

    w_qkv, w_out = next(arriving)
    gains = w_qkv[:, width + 2 * keys : width + 2 * keys + 2].T.astype(F32)
    gain_attn, gain_ffn = gains[0], gains[1]
    entering = own_input.astype(F32)
    middle, normed, _ = run(attention_layer, entering, w_qkv, w_out, gain_attn, gain_ffn, table)
    w_gate, w_up = next(arriving)
    (inner,) = run(functools.partial(feed, kept=False), normed, w_gate, w_up)
    w_down = next(arriving)
    result = run(leave, inner, w_down, middle)
    received = lax.ppermute(result, "section", [(0, 1)])

    entering = jnp.where(first_section, own_input, received).astype(F32)
    middle, normed_two, first = attention_layer(entering, w_qkv, w_out, gain_attn, gain_ffn, table)
    unit_one, inverse_one, normed_one, query, key, value, mixed = first
    unit_two, inverse_two, _ = normed_of(middle, gain_ffn)
    inner, gate, upward = feed(normed_two, w_gate, w_up, True)

    def feed_norm_back(upstream, d_normed):
        return through_norm(upstream.astype(F32), d_normed, unit_two, inverse_two, gain_ffn)

    def attention_norm_back(d_middle, d_normed):
        return through_norm(d_middle, d_normed, unit_one, inverse_one, gain_attn).astype(BF16)

    def heads_back(d_middle):
        d_mixed = back(d_middle.astype(BF16), w_out).astype(BF16)
        return attend_back(d_mixed, query, key, value, table)

    def joined(d_query, d_key, d_value):
        zeros = jnp.zeros((tokens, PAIR), BF16)
        return jnp.concatenate([d_query, d_key, d_value, zeros], axis=1)

    d_gate, d_up = feed_back(own_grad, w_down, gate, upward)
    d_middle = feed_norm_back(own_grad, enter_back(d_gate, d_up, w_gate, w_up))
    d_normed = back(joined(*heads_back(d_middle)), w_qkv)
    given = lax.ppermute(attention_norm_back(d_middle, d_normed), "section", [(1, 0)])
    upstream = jnp.where(first_section, given, own_grad)

    def side_gains(d_normed_one, d_normed_two):
        g_attn = jnp.sum(d_normed_one * unit_one, axis=0).astype(BF16)
        g_ffn = jnp.sum(d_normed_two * unit_two, axis=0).astype(BF16)
        zeros = jnp.zeros((width, PAIR - 2), BF16)
        return jnp.concatenate([g_attn[:, None], g_ffn[:, None], zeros], axis=1)

    if paired:
        own = lax.axis_index("shard")
        replica = lax.axis_index("dp")
        on_middle = (replica == 1) | (replica == 2)
        by_own = lambda value: ordered(value, own)
        d0, d1, g0, g1, u0, u1, o0, q0, q1, s0 = (Chunk(run, on_middle) for _ in range(10))
        run.last = None
        inner_keep, inner_send = by_own(inner)
        normed_keep, normed_send = by_own(normed_two)
        mixed_keep, mixed_send = by_own(mixed)
        first_keep, first_send = by_own(normed_one)
        upstream = run(lambda v: v, upstream)
        cut = width // 2
        d0.terms(inner_keep, inner_send, upstream[:, :cut])
        d0.to_chip()
        d1.terms(inner_keep, inner_send, upstream[:, cut:])
        d1.to_chip()
        d_gate, d_up = run(feed_back, upstream, w_down, gate, upward)
        half = d_gate.shape[1] // 2
        g0.terms(normed_keep, normed_send, d_gate[:, :half])
        g0.to_chip()
        d0.to_middle()
        g1.terms(normed_keep, normed_send, d_gate[:, half:])
        g1.to_chip()
        u0.terms(normed_keep, normed_send, d_up[:, :half])
        u0.to_chip()
        d1.to_middle()
        d0.across()
        u1.terms(normed_keep, normed_send, d_up[:, half:])
        u1.to_chip()
        d_normed_two = run(enter_back, d_gate, d_up, w_gate, w_up)
        d_middle = run(feed_norm_back, upstream, d_normed_two)
        g0.to_middle()
        d1.across()
        d0.outward()
        d_query, d_key, d_value = run(heads_back, d_middle)
        o0.terms(mixed_keep, mixed_send, d_middle.astype(BF16))
        o0.to_chip()
        g1.to_middle()
        g0.across()
        d1.outward()
        q0.terms(first_keep, first_send, d_query[:, :cut])
        q0.to_chip()
        q1.terms(first_keep, first_send, d_query[:, cut:])
        q1.to_chip()
        d_joined = joined(d_query, d_key, d_value)
        d_normed_one = run(back, d_joined, w_qkv)
        u0.to_middle()
        g1.across()
        g0.outward()
        gains_part = run(side_gains, d_normed_one, d_normed_two)
        gains_keep, gains_send = (x.T for x in by_own(gains_part.T))
        d_side = jnp.concatenate([d_key, d_value], axis=1)
        side_send = run(lambda a, b, g: jnp.concatenate([term(a, b), g], axis=1), first_send, d_side, gains_send)
        side_keep = run(lambda a, b, g: jnp.concatenate([term(a, b), g], axis=1), first_keep, d_side, gains_keep)
        s0.given(side_keep, side_send)
        s0.to_chip()
        u1.to_middle()
        u0.across()
        g1.outward()
        result = run(leave, inner, w_down, middle)
        d_hidden = run(attention_norm_back, d_middle, d_normed_one)
        o0.to_middle()
        u1.across()
        u0.outward()
        q0.to_middle()
        o0.across()
        u1.outward()
        q1.to_middle()
        q0.across()
        o0.outward()
        s0.to_middle()
        q1.across()
        q0.outward()
        s0.across()
        q1.outward()
        s0.outward()
        done = [[c.result() for c in group] for group in ((q0, q1), (o0,), (g0, g1), (u0, u1), (d0, d1), (s0,))]
        g_query, g_out, g_gate, g_up, g_down, g_side = (jnp.concatenate(g, axis=1) for g in done)
    else:
        d_gate, d_up = feed_back(upstream, w_down, gate, upward)
        d_normed_two = enter_back(d_gate, d_up, w_gate, w_up)
        d_middle = feed_norm_back(upstream, d_normed_two)
        d_query, d_key, d_value = heads_back(d_middle)
        d_joined = joined(d_query, d_key, d_value)
        d_normed_one = back(d_joined, w_qkv)
        result = leave(inner, w_down, middle)
        d_hidden = attention_norm_back(d_middle, d_normed_one)
        d_side = jnp.concatenate([d_key, d_value], axis=1)
        g_side = jnp.concatenate([term(normed_one, d_side), side_gains(d_normed_one, d_normed_two)], axis=1)
        parts = [
            term(normed_one, d_query),
            term(mixed, d_middle.astype(BF16)),
            term(normed_two, d_gate),
            term(normed_two, d_up),
            term(inner, upstream),
            g_side,
        ]
        parts = [lax.psum_scatter(p, "shard", scatter_dimension=0, tiled=True) for p in parts]
        g_query, g_out, g_gate, g_up, g_down, g_side = (lax.psum(p, "dp").astype(F32) for p in parts)

    grads = (
        g_query,
        g_side[:, :keys],
        g_side[:, keys : 2 * keys],
        g_out,
        g_gate,
        g_up,
        g_down,
        g_side[:, 2 * keys],
        g_side[:, 2 * keys + 1],
    )
    acts = result.reshape(1, seqs, length, width)
    act_grads = d_hidden.reshape(1, seqs, length, width)
    return (acts, act_grads) + tuple(g[None] for g in grads)


def solution(mesh):
    rows = P("section", "shard", None)
    tokens = P(("dp", "shard"), None, None)
    gains = P("section", "shard")
    acts = P("section", ("dp", "shard"), None, None)
    in_specs = (tokens, P(("dp", "shard"), None)) + (rows,) * 7 + (gains, gains, tokens)
    out_specs = (acts, acts) + (rows,) * 7 + (gains, gains)
    return jax.shard_map(body, mesh=mesh, in_specs=in_specs, out_specs=out_specs, check_vma=False)
```
